32 devices in a mesh: gy: 4 (over z), gz: 8 (over y, x, core).
Axes of the slice: x: 2, y: 2, z: 4, core: 2. Of those that a mesh axis runs over, the one named last changes fastest.
Arguments:
- velocity: float32 [3, 32, 64, 128], P(None, 'gy', 'gz'), may hold values from -6 to 6
- offsets: float32 [3, 32768], P(None, ('gy', 'gz')), may hold values from 2 to 6
- marker_slot: int32 [32768], P(('gy', 'gz')), may hold values from 0 to 1
- fibre_links: int32 [2, 32768], P(None, ('gy', 'gz')), may hold values from 0 to 127
- block_owner: int32 [256, 1], P(('gy', 'gz')), may hold values from 0 to 7; in each aligned block of 8 rows (0 to 7, 8 to 15, ...) at most 2 rows name the same one
- block_tiles: int32 [256, 2], P(('gy', 'gz')), may hold values from 0 to 15
Outputs:
- new_velocity: float32 [3, 32, 64, 128], P(None, 'gy', 'gz')
- marker_velocity: float32 [3, 32768], P(None, ('gy', 'gz'))
The draws below stay inside these ranges and needn't reach their ends.
Inputs may be any that keep to these rules, and one draw needn't show every extreme that they name: `block_owner`: of the 8 blocks of one device, at most 2 name the same index; in some device one index is named exactly 2 times. `block_tiles`: tiles are numbered (y, z, x) row-major over the owner's tiles of 8 cells a side; two slots of a block may name the same tile. `fibre_links`: A marker may be its own partner.
All inputs are finite; a program needn't handle non-finite values.
Results may differ from the reference program's by a relative error of at most 0.0003.
Values sent between devices are 32-bit elements; how exact they have to be, the bound alone decides.
A program may use at most 64 MiB of HBM per device.

```python
import math
import jax
import jax.numpy as jnp
import numpy as np
from jax import lax

CY = 8
CZ = 8
NX = 128
BLOCKS_DEV = 8
BLOCK = 128
SLOTS = 2
TILE_SIDE = 8
STEPS = 2
CAP = 2
NY = 32
NZ = 64
BLOCKS = 256
MARKERS = 32768
TILES_DEV = 16
N_GY = 4
N_GZ = 8


def touch_ends(array, stream_key, least, top_value):
    dims = array.shape
    spot = [jax.random.randint(jax.random.fold_in(stream_key, axis), (), 0, dims[axis]) for axis in range(len(dims))]
    array = array.at[tuple(spot)].set(least)
    longest = dims.index(max(dims))
    spot[longest] = (spot[longest] + 1) % dims[longest]
    return array.at[tuple(spot)].set(top_value)


def steps_of(key, dims, split, least, high):
    def one(dim, parts):
        heights = jax.random.uniform(jax.random.fold_in(jax.random.fold_in(key, 6), dim), (parts,), jnp.float32, least / len(split), high / len(split))
        return jnp.repeat(jnp.exp(heights), dims[dim] // parts).reshape((-1,) + (1,) * (len(dims) - dim - 1))

    factor_of = one(*split[0])
    for cut in split[1:]:
        factor_of = factor_of * one(*cut)
    return factor_of


def deal_out(stream_key, own, number, rows, amount, top, most, lean):
    order = jax.random.permutation(stream_key, amount)
    packed, common = shares(amount, rows * top, most, lean, True), shares(amount, rows * top, most, lean, False)
    places = jnp.arange(amount)

    def named(tallies, rotation):
        used = int((tallies > 0).sum())
        fixed = max(1, used // 4)
        shifted = fixed + (places - fixed + rotation * (used - fixed)) % max(1, amount - fixed)
        return jnp.zeros((amount,), jnp.int32).at[order[jnp.where(places < fixed, places, shifted)]].set(jnp.asarray(tallies, jnp.int32))

    tallies = jnp.where(number % 4 == 0, named(packed, number // 4), named(common, number - number // 4 - 1))
    mixed = jax.random.permutation(jax.random.fold_in(own, 3), amount)
    giver, receiver = mixed[0:amount // 2 * 2:2], mixed[1:amount // 2 * 2:2]
    room = jnp.minimum(tallies[giver] - 1, most - tallies[receiver]) // 2
    room = jnp.where((giver == order[0]) | (receiver == order[0]) | (tallies[receiver] == 0), 0, jnp.maximum(room, 0))
    shifted = jax.random.randint(jax.random.fold_in(own, 4), (amount // 2,), 0, 1 << 20) % (room + 1)
    tallies = tallies.at[giver].add(-shifted).at[receiver].add(shifted)
    items = jnp.searchsorted(jnp.cumsum(tallies), jnp.arange(rows * top), side="right").astype(jnp.int32)
    grid = items.reshape(top, rows).T
    grid = grid[jax.random.permutation(jax.random.fold_in(own, 1), rows)]
    rotation = jax.random.randint(jax.random.fold_in(own, 2), (rows, 1), 0, top)
    return jnp.take_along_axis(grid, (jnp.arange(top)[None, :] + rotation) % top, axis=1)


def shares(number_of, total, limit, skew, full):
    portions = [(1 << 20) // math.isqrt(grade ** skew) + 1 for grade in range(1, number_of + 1)]
    largest = limit if full else min(limit, max(-(-total // number_of), total * portions[0] // sum(portions)))
    least = 1 if total - largest >= number_of - 1 else 0
    given, spare = [largest] + [least] * (number_of - 1), total - largest - least * (number_of - 1)
    while spare > 0:
        movable = [i for i in range(1, number_of) if given[i] < largest] or [i for i in range(1, number_of) if given[i] < limit]
        pool, remaining = sum([portions[i] for i in movable]), spare
        for i in movable:
            addition = min(limit - given[i], max(1, remaining * portions[i] // pool), spare)
            given[i] = given[i] + addition
            spare = spare - addition
    return np.array(given)


def bell_draw(key, shape, deviation, bound, pieces=(), held_as=jnp.bfloat16):
    entries = deviation * jax.random.normal(key, shape, jnp.float32)
    if pieces:
        entries = entries * steps_of(key, shape, pieces, -0.22, 0.18)
    return jnp.clip(entries, -bound, bound).astype(held_as)


def setup_inputs(seed: int = 0) -> dict:
    seeds = jax.random.split(jax.random.key(seed), 7)
    velocity = bell_draw(seeds[0], (3, NY, NZ, NX), 1.0, 6.0, ((1, 4), (2, 8)), jnp.float32)
    offsets = jnp.clip(2.0 + 4.0 * jax.random.uniform(seeds[1], (3, MARKERS), jnp.float32) ** steps_of(seeds[1], (3, MARKERS), ((1, 32),), -0.2, 0.2), 2.0, 6.0)
    marker_slot = touch_ends(jax.random.randint(seeds[2], (MARKERS,), 0, SLOTS), jax.random.fold_in(seeds[2], 1), 0, SLOTS - 1).astype(jnp.int32)
    fibre_links = touch_ends(jax.random.randint(seeds[3], (2, MARKERS), 0, BLOCK), jax.random.fold_in(seeds[3], 1), 0, BLOCK - 1).astype(jnp.int32)
    block_owner_keys = jax.random.split(jax.random.fold_in(seeds[4], 1), BLOCKS // BLOCKS_DEV)
    block_owner_turns = jax.random.permutation(jax.random.fold_in(seeds[4], 3), BLOCKS // BLOCKS_DEV)
    block_owner = jax.vmap(lambda own, number: deal_out(jax.random.fold_in(seeds[4], 2), own, number, BLOCKS_DEV, N_GZ, 1, CAP, 1))(block_owner_keys, block_owner_turns).reshape((BLOCKS, 1))
    block_tiles = touch_ends(jax.random.randint(seeds[5], (BLOCKS, SLOTS), 0, TILES_DEV), jax.random.fold_in(seeds[5], 1), 0, TILES_DEV - 1).astype(jnp.int32)
    return {"velocity": velocity, "offsets": offsets, "marker_slot": marker_slot, "fibre_links": fibre_links, "block_owner": block_owner, "block_tiles": block_tiles}


TENSION = 1.0
VISCOUS = 0.125
FORCING = 0.5
HIGHEST = lax.Precision.HIGHEST

def kernel_weights(offset_rows):
    cells = jnp.arange(TILE_SIDE).astype(offset_rows.dtype)
    distance = cells[None, :, None] - offset_rows[:, None, :]
    bump = (1.0 + jnp.cos(0.5 * math.pi * distance)) * 0.25
    return jnp.where(jnp.abs(distance) < 2.0, bump, jnp.zeros_like(bump))

def slot_masks(slot_rows, slot_count, dtype):
    slot_ids = jnp.arange(slot_count).astype(jnp.int32)
    return (slot_rows[:, None, :] == slot_ids[None, :, None]).astype(dtype)

def kernel_planes(offset_rows):
    along_y = kernel_weights(offset_rows[:, 0])
    along_z = kernel_weights(offset_rows[:, 1])
    along_x = kernel_weights(offset_rows[:, 2])
    count = offset_rows.shape[0]
    plane = (along_z[:, :, None, :] * along_x[:, None, :, :]).reshape(count, TILE_SIDE * TILE_SIDE, offset_rows.shape[2])
    return (along_y, plane)

def spread_terms(force_rows, offset_rows, slot_rows, slot_count):
    masks = slot_masks(slot_rows, slot_count, force_rows.dtype)
    along_y, plane = kernel_planes(offset_rows)
    lifted = masks[:, :, None, None, :] * force_rows[:, None, :, None, :] * along_y[:, None, None, :, :]
    terms = jnp.einsum('bkcjm,bnm->bkcjn', lifted, plane, precision=HIGHEST)
    return terms.reshape(force_rows.shape[0], slot_count, 3 * TILE_SIDE ** 3)

def interpolate(tile_values, offset_rows, slot_rows, slot_count):
    masks = slot_masks(slot_rows, slot_count, tile_values.dtype)
    along_y, plane = kernel_planes(offset_rows)
    count = tile_values.shape[0]
    shaped = tile_values.reshape(count, slot_count, 3, TILE_SIDE, TILE_SIDE * TILE_SIDE)
    partial_sums = jnp.einsum('bkcjn,bnm->bkcjm', shaped, plane, precision=HIGHEST)
    return lax.optimization_barrier(jnp.sum(partial_sums * along_y[:, None, None, :, :] * masks[:, :, None, None, :], axis=(1, 3)))

def place_markers(anchor, offset_rows, slot_rows):
    masks = slot_masks(slot_rows, anchor.shape[1], offset_rows.dtype)
    return lax.optimization_barrier(jnp.sum(masks[:, :, None, :] * anchor[:, :, :, None], axis=1)) + offset_rows

def fibre_force(position, link_rows):
    total = jnp.zeros_like(position)
    for partner_side in range(2):
        partner_index = jnp.broadcast_to(link_rows[partner_side][:, None, :], position.shape)
        delta = jnp.take_along_axis(position, partner_index, axis=2) - position
        length = jnp.sqrt(lax.optimization_barrier(jnp.sum(delta * delta, axis=1, keepdims=True)))
        total = total + TENSION * delta / jnp.maximum(length, 1.0)
    return total

def to_tiles(field):
    comps, span_y, span_z, span_x = field.shape
    side = TILE_SIDE
    shaped = field.reshape(comps, span_y // side, side, span_z // side, side, span_x // side, side)
    shaped = shaped.transpose(1, 3, 5, 0, 2, 4, 6)
    return shaped.reshape(span_y // side * (span_z // side) * (span_x // side), comps * side ** 3)

def from_tiles(tiles, span_y, span_z, span_x):
    side = TILE_SIDE
    shaped = tiles.reshape(span_y // side, span_z // side, span_x // side, 3, side, side, side)
    return shaped.transpose(3, 0, 4, 1, 5, 2, 6).reshape(3, span_y, span_z, span_x)

def laplace(field):
    padded = jnp.pad(field, ((0, 0), (0, 0), (0, 0), (1, 1)))
    beside_all = jnp.roll(field, 1, 1) + jnp.roll(field, -1, 1) + jnp.roll(field, 1, 2) + jnp.roll(field, -1, 2)
    return beside_all + padded[..., 2:] + padded[..., :-2] - 6.0 * field

def reference(velocity, offsets, marker_slot, fibre_links, block_owner, block_tiles):
    groups = N_GY * N_GZ
    tiles_y = CY // TILE_SIDE
    tiles_z = CZ // TILE_SIDE
    tiles_x = NX // TILE_SIDE
    tile_len = 3 * TILE_SIDE ** 3
    offs_all = offsets.reshape(3, groups, BLOCKS_DEV, BLOCK).transpose(1, 2, 0, 3)
    slot_all = marker_slot.reshape(groups, BLOCKS_DEV, BLOCK)
    link_all = fibre_links.reshape(2, groups, BLOCKS_DEV, BLOCK).transpose(1, 0, 2, 3)
    owner_all = block_owner.reshape(groups, BLOCKS_DEV)
    tiles_all = block_tiles.reshape(groups, BLOCKS_DEV, SLOTS)
    grid_rows = (jnp.arange(groups) // N_GZ).astype(jnp.int32)

    def spread_group(total, item):
        offset_rows, slot_rows, link_rows, owner_ids, tile_ids, grid_row = item
        tile_y = tile_ids // (tiles_z * tiles_x)
        tile_z = tile_ids // tiles_x % tiles_z
        tile_x = tile_ids % tiles_x
        anchor = jnp.stack([grid_row * CY + tile_y * TILE_SIDE, owner_ids[:, None] * CZ + tile_z * TILE_SIDE, tile_x * TILE_SIDE], axis=-1).astype(offsets.dtype)
        where_tile = (((grid_row * tiles_y + tile_y) * (N_GZ * tiles_z) + owner_ids[:, None] * tiles_z + tile_z) * tiles_x + tile_x).astype(jnp.int32)
        position = place_markers(anchor, offset_rows, slot_rows)
        force_rows = fibre_force(position, link_rows)
        terms = spread_terms(force_rows, offset_rows, slot_rows, SLOTS)
        return (total.at[where_tile.reshape(-1)].add(terms.reshape(-1, tile_len)), where_tile)
    blank = jnp.zeros((NY // TILE_SIDE * (NZ // TILE_SIDE) * tiles_x, tile_len), offsets.dtype)
    force_tiles, where_all = lax.scan(spread_group, blank, (offs_all, slot_all, link_all, owner_all, tiles_all, grid_rows))
    spread = from_tiles(force_tiles, NY, NZ, NX)
    field = velocity
    for substep in range(STEPS):
        field = field + VISCOUS * laplace(field) + FORCING * spread
    velocity_tiles = to_tiles(field)

    def sample_group(item):
        offset_rows, slot_rows, where_tile = item
        return interpolate(velocity_tiles[where_tile], offset_rows, slot_rows, SLOTS)
    sampled = lax.map(sample_group, (offs_all, slot_all, where_all))
    marker_velocity = sampled.transpose(2, 0, 1, 3).reshape(3, MARKERS)
    return (field, marker_velocity)
```

```python
import functools
import math

import jax
import jax.numpy as jnp
from jax import lax
from jax.experimental import pallas as pl
from jax.experimental.pallas import tpu as pltpu
from jax.sharding import PartitionSpec as P

BLOCK = 128
SIDE = 8
VISCOUS = 0.125
FORCING = 0.5
MESH = pl.DeviceIdType.MESH
F32 = jnp.float32
BF16 = jnp.bfloat16


def split(x):
    hi = x.astype(BF16)
    return hi, (x - hi.astype(F32)).astype(BF16)


def cos_sin(offset):
    u = jnp.floor(offset + 0.5)
    a = (offset - u) * (0.5 * math.pi)
    u = u - 4.0
    z = a * a
    s = a * (1.0 + z * (-1 / 6 + z * (1 / 120 + z * (-1 / 5040 + z * (1 / 362880)))))
    c = 1.0 + z * (-0.5 + z * (1 / 24 + z * (-1 / 720 + z * (1 / 40320 - z * (1 / 3628800)))))
    w = jnp.abs(u)
    cq = 1.0 - w
    sq = u * (2.0 - w)
    return cq * c - sq * s, sq * c + cq * s


def diffuse(f, ylo, yhi, zlo, zhi):
    shape = f.shape
    z = lax.broadcasted_iota(jnp.int32, shape, 2)
    x = lax.broadcasted_iota(jnp.int32, shape, 3)
    y_down = jnp.concatenate([ylo, f[:, :-1]], axis=1)
    y_up = jnp.concatenate([f[:, 1:], yhi], axis=1)
    z_down = jnp.where(z == 0, jnp.broadcast_to(zlo, shape), pltpu.roll(f, 1, 2))
    z_up = jnp.where(z == shape[2] - 1, jnp.broadcast_to(zhi, shape), pltpu.roll(f, shape[2] - 1, 2))
    x_down = jnp.where(x == 0, 0.0, pltpu.roll(f, 1, 3))
    x_up = jnp.where(x == shape[3] - 1, 0.0, pltpu.roll(f, shape[3] - 1, 3))
    beside = (y_down + y_up) + (z_down + z_up) + (x_down + x_up)
    return f + VISCOUS * (beside - 6.0 * f)


def kernel(
    rows, peers, cap,
    v_ref, off_ref, slot_ref, link_ref, owner_ref, tile_ref,
    nv_ref, mv_ref,
    stage, sendb, recvb, px_ref, w_ref, retsend, retrecv, f1_ref, hy, hz, gy_, gz_,
    m_send, m_recv, r_send, r_recv, h_send, h_recv, g_send, g_recv,
):
    me_y, me = lax.axis_index("gy"), lax.axis_index("gz")
    y_next, y_prev = lax.rem(me_y + 1, rows), lax.rem(me_y + rows - 1, rows)
    z_next, z_prev = lax.rem(me + 1, peers), lax.rem(me + peers - 1, peers)
    ahead = [lax.rem(me + d, peers) for d in range(peers)]
    behind = [lax.rem(me + peers - d, peers) for d in range(peers)]
    nb = owner_ref.shape[0]
    nx = v_ref.shape[3]

    barrier = pltpu.get_barrier_semaphore()
    for d in range(1, peers):
        pl.semaphore_signal(barrier, inc=1, device_id=(me_y, ahead[d]), device_id_type=MESH)
    for other in (y_next, y_prev):
        pl.semaphore_signal(barrier, inc=1, device_id=(other, me), device_id_type=MESH)

    def by_block(ref, row):
        return jnp.concatenate(
            [ref[row : row + 1, b * BLOCK : (b + 1) * BLOCK] for b in range(nb)], axis=0
        )

    offs = [by_block(off_ref, r) for r in range(3)]
    owner = jnp.broadcast_to(owner_ref[...], (nb, BLOCK))
    tile_x = jnp.where(
        slot_ref[...] == 0,
        jnp.broadcast_to(tile_ref[:, 0:1], (nb, BLOCK)),
        jnp.broadcast_to(tile_ref[:, 1:2], (nb, BLOCK)),
    )
    first_x = (tile_x * SIDE).astype(F32)
    position = [
        (me_y * SIDE).astype(F32) + offs[0],
        (owner * SIDE).astype(F32) + offs[1],
        first_x + offs[2],
    ]
    force = [jnp.zeros((nb, BLOCK), F32) for _ in range(3)]
    for side in range(2):
        partner = by_block(link_ref, side)
        delta = [
            jnp.take_along_axis(p, partner, axis=1, mode="promise_in_bounds") - p for p in position
        ]
        length = jnp.sqrt(delta[0] * delta[0] + delta[1] * delta[1] + delta[2] * delta[2])
        scale = jnp.maximum(length, 1.0)
        force = [f + dl / scale for f, dl in zip(force, delta)]
    sub = lax.broadcasted_iota(jnp.int32, (nb, BLOCK), 0)
    rank = jnp.zeros((nb, BLOCK), jnp.int32)
    for b in range(nb - 1):
        same = jnp.broadcast_to(owner[b : b + 1], (nb, BLOCK)) == owner
        rank = rank + jnp.where(same & (sub > b), 1, 0)
    key = owner * cap + rank

    for r, row in enumerate(offs + [first_x] + force + [jnp.zeros((nb, BLOCK), F32)]):
        stage[r] = row
    blocks = [stage[:, b, :] for b in range(nb)]
    keys = [jnp.broadcast_to(key[b : b + 1], (8, BLOCK)) for b in range(nb)]
    for d in range(peers):
        for k in range(cap):
            acc = jnp.zeros((8, BLOCK), F32)
            for b in range(nb):
                acc = jnp.where(keys[b] == ahead[d] * cap + k, blocks[b], acc)
            if d == 0:
                recvb[0, k] = acc
            else:
                sendb[d, k] = acc

    def faces(src, ybuf, zbuf, send, recv):
        last = SIDE - 1
        pairs = [
            (src.at[:, pl.ds(last, 1)], ybuf.at[:, pl.ds(0, 1)], (y_next, me)),
            (src.at[:, pl.ds(0, 1)], ybuf.at[:, pl.ds(1, 1)], (y_prev, me)),
            (src.at[:, :, pl.ds(last, 1)], zbuf.at[:, :, pl.ds(last, 1)], (me_y, z_next)),
            (src.at[:, :, pl.ds(0, 1)], zbuf.at[:, :, pl.ds(0, 1)], (me_y, z_prev)),
        ]
        return [
            pltpu.make_async_remote_copy(
                src_ref=a, dst_ref=b, send_sem=send.at[i], recv_sem=recv.at[i],
                device_id=to, device_id_type=MESH,
            )
            for i, (a, b, to) in enumerate(pairs)
        ]

    def layers(ybuf, zbuf):
        last = SIDE - 1
        return ybuf[:, 0:1], ybuf[:, 1:2], zbuf[:, :, last : last + 1], zbuf[:, :, 0:1]

    pl.semaphore_wait(barrier, peers + 1)
    outgoing = []
    for d in range(1, peers):
        copy = pltpu.make_async_remote_copy(
            src_ref=sendb.at[d], dst_ref=recvb.at[d], send_sem=m_send.at[d], recv_sem=m_recv.at[d],
            device_id=(me_y, ahead[d]), device_id_type=MESH,
        )
        copy.start()
        outgoing.append(copy)
    halo = faces(v_ref, hy, hz, h_send, h_recv)
    for copy in halo:
        copy.start()

    cell = lax.broadcasted_iota(jnp.int32, (SIDE, BLOCK), 0)
    cell_f = cell.astype(F32)
    quarter = cell % 4
    cos_cell = jnp.where(quarter == 0, 0.25, jnp.where(quarter == 2, -0.25, 0.0))
    sin_cell = jnp.where(quarter == 1, 0.25, jnp.where(quarter == 3, -0.25, 0.0))
    wide = jnp.zeros((3 * SIDE * SIDE, 2 * nx), F32)
    narrow = jnp.zeros((3 * SIDE * SIDE, nx), F32)
    nt = (((1,), (1,)), ((), ()))
    for d in range(peers):
        if d > 0:
            outgoing[d - 1].wait_recv()
        his, los = [], []
        for k in range(cap):
            data = recvb[d, k]
            cosines, sines = cos_sin(data)
            weights = []
            for r in range(3):
                near = jnp.abs(cell_f - data[r : r + 1]) < 2.0
                bump = 0.25 + (cos_cell * cosines[r : r + 1] + sin_cell * sines[r : r + 1])
                weights.append(jnp.where(near, bump, 0.0))
            wy, wz, wx = weights
            plane = jnp.concatenate([wy[y : y + 1] * wz for y in range(SIDE)], axis=0)
            w_ref[d, k] = plane
            lifted = jnp.concatenate([data[4 + c : 5 + c] * plane for c in range(3)], axis=0)
            hi, lo = split(lifted)
            his.append(hi)
            los.append(lo)
            wx_hi = wx.astype(BF16).astype(F32)
            wx_lo = wx - wx_hi
            start = jnp.broadcast_to(data[3:4], (SIDE, BLOCK))
            spots = [start == float(SIDE * t) for t in range(nx // SIDE)]
            for part, piece in enumerate((wx_hi, wx_lo)):
                full = jnp.concatenate([jnp.where(s, piece, 0.0) for s in spots], axis=0)
                px_ref[d, part * nx : (part + 1) * nx, k * BLOCK : (k + 1) * BLOCK] = full.astype(BF16)
        hi = jnp.concatenate(his, axis=1)
        lo = jnp.concatenate(los, axis=1)
        wide = wide + lax.dot_general(hi, px_ref[d], nt, preferred_element_type=F32)
        narrow = narrow + lax.dot_general(lo, px_ref[d, :nx], nt, preferred_element_type=F32)
    spread = (FORCING * (wide[:, :nx] + (wide[:, nx:] + narrow))).reshape(3, SIDE, SIDE, nx)

    for copy in halo:
        copy.wait_recv()
    f1 = diffuse(v_ref[...], *layers(hy, hz)) + spread
    f1_ref[...] = f1
    halo1 = faces(f1_ref, gy_, gz_, g_send, g_recv)
    for copy in halo1:
        copy.start()
    for copy in halo1:
        copy.wait_recv()
    f2 = diffuse(f1, *layers(gy_, gz_)) + spread
    nv_ref[...] = f2

    hi, lo = split(f2.reshape(3 * SIDE * SIDE, nx))
    hihi = jnp.concatenate([hi, hi], axis=1)
    back = []
    for d in list(range(1, peers)) + [0]:
        got = jnp.dot(hihi, px_ref[d], preferred_element_type=F32) + jnp.dot(
            lo, px_ref[d, :nx], preferred_element_type=F32
        )
        lines = []
        for k in range(cap):
            plane = w_ref[d, k]
            for c in range(3):
                part = got[c * 64 : (c + 1) * 64, k * BLOCK : (k + 1) * BLOCK] * plane
                lines.append(jnp.sum(part, axis=0, keepdims=True))
        lines.append(jnp.zeros((8 - 3 * cap, BLOCK), F32))
        result = jnp.concatenate(lines, axis=0)
        if d == 0:
            retrecv[0] = result
        else:
            retsend[d] = result
            copy = pltpu.make_async_remote_copy(
                src_ref=retsend.at[d], dst_ref=retrecv.at[d],
                send_sem=r_send.at[d], recv_sem=r_recv.at[d],
                device_id=(me_y, behind[d]), device_id_type=MESH,
            )
            copy.start()
            back.append(copy)
    for copy in back:
        copy.wait_recv()
    arrived = [retrecv[d] for d in range(peers)]
    for b in range(nb):
        mine = jnp.broadcast_to(owner[b : b + 1], (8, BLOCK))
        acc = jnp.zeros((8, BLOCK), F32)
        for d in range(peers):
            acc = jnp.where(mine == ahead[d], arrived[d], acc)
        second = jnp.broadcast_to(rank[b : b + 1], (3, BLOCK)) == 1
        mv_ref[:, b * BLOCK : (b + 1) * BLOCK] = jnp.where(second, acc[3:6], acc[0:3])
    for copy in outgoing + halo + halo1 + back:
        copy.wait_send()


def local(rows, peers, velocity, offsets, marker_slot, fibre_links, block_owner, block_tiles):
    nb = block_owner.shape[0]
    cap = max(2, 2 * nb // peers)
    nx = velocity.shape[3]
    assert velocity.shape[1:3] == (SIDE, SIDE) and nb == 8 and cap == 2
    vmem = pl.BlockSpec(memory_space=pltpu.VMEM)
    dma = pltpu.SemaphoreType.DMA
    return pl.pallas_call(
        functools.partial(kernel, rows, peers, cap),
        out_shape=(
            jax.ShapeDtypeStruct(velocity.shape, F32),
            jax.ShapeDtypeStruct(offsets.shape, F32),
        ),
        in_specs=[vmem] * 6,
        out_specs=(vmem, vmem),
        scratch_shapes=[
            pltpu.VMEM((8, nb, BLOCK), F32),
            pltpu.VMEM((peers, cap, 8, BLOCK), F32),
            pltpu.VMEM((peers, cap, 8, BLOCK), F32),
            pltpu.VMEM((peers, 2 * nx, cap * BLOCK), BF16),
            pltpu.VMEM((peers, cap, SIDE * SIDE, BLOCK), F32),
            pltpu.VMEM((peers, 8, BLOCK), F32),
            pltpu.VMEM((peers, 8, BLOCK), F32),
            pltpu.VMEM((3, SIDE, SIDE, nx), F32),
            pltpu.VMEM((3, 2, SIDE, nx), F32),
            pltpu.VMEM((3, SIDE, SIDE, nx), F32),
            pltpu.VMEM((3, 2, SIDE, nx), F32),
            pltpu.VMEM((3, SIDE, SIDE, nx), F32),
            dma((peers,)), dma((peers,)), dma((peers,)), dma((peers,)),
            dma((4,)), dma((4,)), dma((4,)), dma((4,)),
        ],
        compiler_params=pltpu.CompilerParams(collective_id=0, has_side_effects=True),
    )(
        velocity, offsets, marker_slot.reshape(nb, BLOCK), fibre_links, block_owner, block_tiles
    )


def solution(mesh):
    return jax.shard_map(
        functools.partial(local, mesh.shape["gy"], mesh.shape["gz"]),
        mesh=mesh,
        in_specs=(
            P(None, "gy", "gz", None),
            P(None, ("gy", "gz")),
            P(("gy", "gz")),
            P(None, ("gy", "gz")),
            P(("gy", "gz"), None),
            P(("gy", "gz"), None),
        ),
        out_specs=(P(None, "gy", "gz", None), P(None, ("gy", "gz"))),
        check_vma=False,
    )
```

```python
import functools
import math

import jax
import jax.numpy as jnp
from jax import lax
from jax.experimental import pallas as pl
from jax.experimental.pallas import tpu as pltpu
from jax.sharding import PartitionSpec as P

BLOCK = 128
SIDE = 8
VISCOUS = 0.125
FORCING = 0.5
MESH = pl.DeviceIdType.MESH
F32 = jnp.float32
BF16 = jnp.bfloat16


def split(x):
    hi = x.astype(BF16)
    return hi, (x - hi.astype(F32)).astype(BF16)


def cos_sin(offset):
    u = jnp.floor(offset + 0.5)
    a = (offset - u) * (0.5 * math.pi)
    u = u - 4.0
    z = a * a
    s = a * (1.0 + z * (-1 / 6 + z * (1 / 120 + z * (-1 / 5040 + z * (1 / 362880)))))
    c = 1.0 + z * (-0.5 + z * (1 / 24 + z * (-1 / 720 + z * (1 / 40320 - z * (1 / 3628800)))))
    w = jnp.abs(u)
    cq = 1.0 - w
    sq = u * (2.0 - w)
    return cq * c - sq * s, sq * c + cq * s


def diffuse(f, ylo, yhi, zlo, zhi):
    shape = f.shape
    z = lax.broadcasted_iota(jnp.int32, shape, 2)
    x = lax.broadcasted_iota(jnp.int32, shape, 3)
    y_down = jnp.concatenate([ylo, f[:, :-1]], axis=1)
    y_up = jnp.concatenate([f[:, 1:], yhi], axis=1)
    z_down = jnp.where(z == 0, jnp.broadcast_to(zlo, shape), pltpu.roll(f, 1, 2))
    z_up = jnp.where(z == shape[2] - 1, jnp.broadcast_to(zhi, shape), pltpu.roll(f, shape[2] - 1, 2))
    x_down = jnp.where(x == 0, 0.0, pltpu.roll(f, 1, 3))
    x_up = jnp.where(x == shape[3] - 1, 0.0, pltpu.roll(f, shape[3] - 1, 3))
    beside = (y_down + y_up) + (z_down + z_up) + (x_down + x_up)
    return f + VISCOUS * (beside - 6.0 * f)


def kernel(
    rows, peers, cap,
    v_ref, off_ref, slot_ref, link_ref, owner_ref, tile_ref,
    nv_ref, mv_ref,
    stage, sendb, recvb, px_ref, w_ref, retsend, retrecv, f1_ref, hy, hz, gy_, gz_,
    m_send, m_recv, r_send, r_recv, h_send, h_recv, g_send, g_recv,
):
    me_y, me = lax.axis_index("gy"), lax.axis_index("gz")
    y_next, y_prev = lax.rem(me_y + 1, rows), lax.rem(me_y + rows - 1, rows)
    z_next, z_prev = lax.rem(me + 1, peers), lax.rem(me + peers - 1, peers)
    ahead = [lax.rem(me + d, peers) for d in range(peers)]
    behind = [lax.rem(me + peers - d, peers) for d in range(peers)]
    nb = owner_ref.shape[1]
    nx = v_ref.shape[3]

    barrier = pltpu.get_barrier_semaphore()
    for d in range(1, peers):
        pl.semaphore_signal(barrier, inc=1, device_id=(me_y, ahead[d]), device_id_type=MESH)
    for other in (y_next, y_prev):
        pl.semaphore_signal(barrier, inc=1, device_id=(other, me), device_id_type=MESH)

    def by_block(ref, row):
        return jnp.concatenate(
            [ref[row : row + 1, b * BLOCK : (b + 1) * BLOCK] for b in range(nb)], axis=0
        )

    own_row = lax.broadcasted_iota(jnp.int32, (nb, nb), 0) == lax.broadcasted_iota(
        jnp.int32, (nb, nb), 1
    )

    def column(row):
        spread_row = jnp.broadcast_to(row.astype(F32), (nb, nb))
        total = jnp.sum(jnp.where(own_row, spread_row, 0.0), axis=1, keepdims=True)
        return jnp.broadcast_to(total, (nb, BLOCK)).astype(jnp.int32)

    offs = [by_block(off_ref, r) for r in range(3)]
    owner = column(owner_ref[...])
    tile_x = jnp.where(
        slot_ref[...] == 0,
        column(tile_ref[0:1]),
        column(tile_ref[1:2]),
    )
    first_x = (tile_x * SIDE).astype(F32)
    position = [
        (me_y * SIDE).astype(F32) + offs[0],
        (owner * SIDE).astype(F32) + offs[1],
        first_x + offs[2],
    ]
    force = [jnp.zeros((nb, BLOCK), F32) for _ in range(3)]
    for side in range(2):
        partner = by_block(link_ref, side)
        delta = [
            jnp.take_along_axis(p, partner, axis=1, mode="promise_in_bounds") - p for p in position
        ]
        length = jnp.sqrt(delta[0] * delta[0] + delta[1] * delta[1] + delta[2] * delta[2])
        scale = jnp.maximum(length, 1.0)
        force = [f + dl / scale for f, dl in zip(force, delta)]
    sub = lax.broadcasted_iota(jnp.int32, (nb, BLOCK), 0)
    rank = jnp.zeros((nb, BLOCK), jnp.int32)
    for b in range(nb - 1):
        same = jnp.broadcast_to(owner[b : b + 1], (nb, BLOCK)) == owner
        rank = rank + jnp.where(same & (sub > b), 1, 0)
    key = owner * cap + rank

    for r, row in enumerate(offs + [first_x] + force + [jnp.zeros((nb, BLOCK), F32)]):
        stage[r] = row
    blocks = [stage[:, b, :] for b in range(nb)]
    keys = [jnp.broadcast_to(key[b : b + 1], (8, BLOCK)) for b in range(nb)]
    for d in range(peers):
        for k in range(cap):
            acc = jnp.zeros((8, BLOCK), F32)
            for b in range(nb):
                acc = jnp.where(keys[b] == ahead[d] * cap + k, blocks[b], acc)
            if d == 0:
                recvb[0, k] = acc
            else:
                sendb[d, k] = acc

    def faces(src, ybuf, zbuf, send, recv):
        last = SIDE - 1
        pairs = [
            (src.at[:, pl.ds(last, 1)], ybuf.at[:, pl.ds(0, 1)], (y_next, me)),
            (src.at[:, pl.ds(0, 1)], ybuf.at[:, pl.ds(1, 1)], (y_prev, me)),
            (src.at[:, :, pl.ds(last, 1)], zbuf.at[:, :, pl.ds(last, 1)], (me_y, z_next)),
            (src.at[:, :, pl.ds(0, 1)], zbuf.at[:, :, pl.ds(0, 1)], (me_y, z_prev)),
        ]
        return [
            pltpu.make_async_remote_copy(
                src_ref=a, dst_ref=b, send_sem=send.at[i], recv_sem=recv.at[i],
                device_id=to, device_id_type=MESH,
            )
            for i, (a, b, to) in enumerate(pairs)
        ]

    def layers(ybuf, zbuf):
        last = SIDE - 1
        return ybuf[:, 0:1], ybuf[:, 1:2], zbuf[:, :, last : last + 1], zbuf[:, :, 0:1]

    pl.semaphore_wait(barrier, peers + 1)
    outgoing = []
    for d in range(1, peers):
        copy = pltpu.make_async_remote_copy(
            src_ref=sendb.at[d], dst_ref=recvb.at[d], send_sem=m_send.at[d], recv_sem=m_recv.at[d],
            device_id=(me_y, ahead[d]), device_id_type=MESH,
        )
        copy.start()
        outgoing.append(copy)
    halo = faces(v_ref, hy, hz, h_send, h_recv)
    for copy in halo:
        copy.start()

    cell = lax.broadcasted_iota(jnp.int32, (SIDE, BLOCK), 0)
    cell_f = cell.astype(F32)
    quarter = cell % 4
    cos_cell = jnp.where(quarter == 0, 0.25, jnp.where(quarter == 2, -0.25, 0.0))
    sin_cell = jnp.where(quarter == 1, 0.25, jnp.where(quarter == 3, -0.25, 0.0))
    wide = jnp.zeros((3 * SIDE * SIDE, 2 * nx), F32)
    narrow = jnp.zeros((3 * SIDE * SIDE, nx), F32)
    nt = (((1,), (1,)), ((), ()))
    for d in range(peers):
        if d == 1:
            for copy in halo:
                copy.wait_recv()
            f1_ref[...] = diffuse(v_ref[...], *layers(hy, hz))
        if d > 0:
            outgoing[d - 1].wait_recv()
        his, los = [], []
        for k in range(cap):
            data = recvb[d, k]
            cosines, sines = cos_sin(data)
            weights = []
            for r in range(3):
                near = jnp.abs(cell_f - data[r : r + 1]) < 2.0
                bump = 0.25 + (cos_cell * cosines[r : r + 1] + sin_cell * sines[r : r + 1])
                weights.append(jnp.where(near, bump, 0.0))
            wy, wz, wx = weights
            plane = jnp.concatenate([wy[y : y + 1] * wz for y in range(SIDE)], axis=0)
            w_ref[d, k] = plane
            lifted = jnp.concatenate([data[4 + c : 5 + c] * plane for c in range(3)], axis=0)
            hi, lo = split(lifted)
            his.append(hi)
            los.append(lo)
            wx_hi = wx.astype(BF16).astype(F32)
            wx_lo = wx - wx_hi
            start = jnp.broadcast_to(data[3:4], (SIDE, BLOCK))
            spots = [start == float(SIDE * t) for t in range(nx // SIDE)]
            for part, piece in enumerate((wx_hi, wx_lo)):
                full = jnp.concatenate([jnp.where(s, piece, 0.0) for s in spots], axis=0)
                px_ref[d, part * nx : (part + 1) * nx, k * BLOCK : (k + 1) * BLOCK] = full.astype(BF16)
        hi = jnp.concatenate(his, axis=1)
        lo = jnp.concatenate(los, axis=1)
        wide = wide + lax.dot_general(hi, px_ref[d], nt, preferred_element_type=F32)
        narrow = narrow + lax.dot_general(lo, px_ref[d, :nx], nt, preferred_element_type=F32)
    spread = (FORCING * (wide[:, :nx] + (wide[:, nx:] + narrow))).reshape(3, SIDE, SIDE, nx)

    f1 = f1_ref[...] + spread
    f1_ref[...] = f1
    halo1 = faces(f1_ref, gy_, gz_, g_send, g_recv)
    for copy in halo1:
        copy.start()
    for copy in halo1:
        copy.wait_recv()
    f2 = diffuse(f1, *layers(gy_, gz_)) + spread
    nv_ref[...] = f2

    hi, lo = split(f2.reshape(3 * SIDE * SIDE, nx))
    hihi = jnp.concatenate([hi, hi], axis=1)
    back = []
    for d in list(range(1, peers)) + [0]:
        got = jnp.dot(hihi, px_ref[d], preferred_element_type=F32) + jnp.dot(
            lo, px_ref[d, :nx], preferred_element_type=F32
        )
        lines = []
        for k in range(cap):
            plane = w_ref[d, k]
            for c in range(3):
                part = got[c * 64 : (c + 1) * 64, k * BLOCK : (k + 1) * BLOCK] * plane
                lines.append(jnp.sum(part, axis=0, keepdims=True))
        lines.append(jnp.zeros((8 - 3 * cap, BLOCK), F32))
        result = jnp.concatenate(lines, axis=0)
        if d == 0:
            retrecv[0] = result
        else:
            retsend[d] = result
            copy = pltpu.make_async_remote_copy(
                src_ref=retsend.at[d], dst_ref=retrecv.at[d],
                send_sem=r_send.at[d], recv_sem=r_recv.at[d],
                device_id=(me_y, behind[d]), device_id_type=MESH,
            )
            copy.start()
            back.append(copy)
    for copy in back:
        copy.wait_recv()
    arrived = [retrecv[d] for d in range(peers)]
    for b in range(nb):
        mine = jnp.broadcast_to(owner[b : b + 1], (8, BLOCK))
        acc = jnp.zeros((8, BLOCK), F32)
        for d in range(peers):
            acc = jnp.where(mine == ahead[d], arrived[d], acc)
        second = jnp.broadcast_to(rank[b : b + 1], (3, BLOCK)) == 1
        mv_ref[:, b * BLOCK : (b + 1) * BLOCK] = jnp.where(second, acc[3:6], acc[0:3])
    for copy in outgoing + halo + halo1 + back:
        copy.wait_send()


def local(rows, peers, velocity, offsets, marker_slot, fibre_links, block_owner, block_tiles):
    nb = block_owner.shape[0]
    cap = max(2, 2 * nb // peers)
    nx = velocity.shape[3]
    assert velocity.shape[1:3] == (SIDE, SIDE) and nb == 8 and cap == 2
    vmem = pl.BlockSpec(memory_space=pltpu.VMEM)
    dma = pltpu.SemaphoreType.DMA
    return pl.pallas_call(
        functools.partial(kernel, rows, peers, cap),
        out_shape=(
            jax.ShapeDtypeStruct(velocity.shape, F32),
            jax.ShapeDtypeStruct(offsets.shape, F32),
        ),
        in_specs=[vmem] * 6,
        out_specs=(vmem, vmem),
        scratch_shapes=[
            pltpu.VMEM((8, nb, BLOCK), F32),
            pltpu.VMEM((peers, cap, 8, BLOCK), F32),
            pltpu.VMEM((peers, cap, 8, BLOCK), F32),
            pltpu.VMEM((peers, 2 * nx, cap * BLOCK), BF16),
            pltpu.VMEM((peers, cap, SIDE * SIDE, BLOCK), F32),
            pltpu.VMEM((peers, 8, BLOCK), F32),
            pltpu.VMEM((peers, 8, BLOCK), F32),
            pltpu.VMEM((3, SIDE, SIDE, nx), F32),
            pltpu.VMEM((3, 2, SIDE, nx), F32),
            pltpu.VMEM((3, SIDE, SIDE, nx), F32),
            pltpu.VMEM((3, 2, SIDE, nx), F32),
            pltpu.VMEM((3, SIDE, SIDE, nx), F32),
            dma((peers,)), dma((peers,)), dma((peers,)), dma((peers,)),
            dma((4,)), dma((4,)), dma((4,)), dma((4,)),
        ],
        compiler_params=pltpu.CompilerParams(collective_id=0, has_side_effects=True),
    )(
        velocity, offsets, marker_slot.reshape(nb, BLOCK), fibre_links, block_owner.T, block_tiles.T
    )


def solution(mesh):
    return jax.shard_map(
        functools.partial(local, mesh.shape["gy"], mesh.shape["gz"]),
        mesh=mesh,
        in_specs=(
            P(None, "gy", "gz", None),
            P(None, ("gy", "gz")),
            P(("gy", "gz")),
            P(None, ("gy", "gz")),
            P(("gy", "gz"), None),
            P(("gy", "gz"), None),
        ),
        out_specs=(P(None, "gy", "gz", None), P(None, ("gy", "gz"))),
        check_vma=False,
    )
```
